32 devices in a mesh: rep: 4 (over y, x), fsdp: 8 (over z, core).
Axes of the slice: x: 2, y: 2, z: 4, core: 2. Of those that a mesh axis runs over, the one named last changes fastest.
Arguments:
- tokens: bfloat16 [4096, 1600], P(('rep', 'fsdp')), may hold values from -6 to 6
- doc_starts: int32 [4, 3], P('rep'), may hold values from 0 to 1023, as said below
- pic_starts: int32 [4, 1], P('rep'), may hold values from 0 to 768, as said below
- ln1_gain: bfloat16 [1600], P('fsdp'), may hold values from 0.099609375 to 1.8984375
- ln1_shift: bfloat16 [1600], P('fsdp'), may hold values from -3 to 3
- w_qkv: bfloat16 [1600, 4800], P('fsdp'), may hold values from -0.15625 to 0.15625
- bias_qv: bfloat16 [3200], P('fsdp'), may hold values from -3 to 3
- w_attn: bfloat16 [1600, 1600], P('fsdp'), may hold values from -2.5 to 2.5
- bias_attn: bfloat16 [1600], P('fsdp'), may hold values from -3 to 3
- ln2_gain: bfloat16 [1600], P('fsdp'), may hold values from 0.099609375 to 1.8984375
- ln2_shift: bfloat16 [1600], P('fsdp'), may hold values from -3 to 3
- w_fc: bfloat16 [1600, 6400], P('fsdp'), may hold values from -0.15625 to 0.15625
- bias_fc: bfloat16 [6400], P('fsdp'), may hold values from -3 to 3
- w_proj: bfloat16 [6400, 1600], P('fsdp'), may hold values from -0.078125 to 0.078125
- bias_proj: bfloat16 [1600], P('fsdp'), may hold values from -3 to 3
- cotangent: bfloat16 [4096, 1600], P(('rep', 'fsdp')), may hold values from -6 to 6
Outputs:
- output: bfloat16 [4096, 1600], P(('rep', 'fsdp'))
- tokens_grad: bfloat16 [4096, 1600], P(('rep', 'fsdp'))
- ln1_gain_grad: float32 [1600], P('fsdp')
- ln1_shift_grad: float32 [1600], P('fsdp')
- w_qkv_grad: float32 [1600, 4800], P('fsdp')
- bias_qv_grad: float32 [3200], P('fsdp')
- w_attn_grad: float32 [1600, 1600], P('fsdp')
- bias_attn_grad: float32 [1600], P('fsdp')
- ln2_gain_grad: float32 [1600], P('fsdp')
- ln2_shift_grad: float32 [1600], P('fsdp')
- w_fc_grad: float32 [1600, 6400], P('fsdp')
- bias_fc_grad: float32 [6400], P('fsdp')
- w_proj_grad: float32 [6400, 1600], P('fsdp')
- bias_proj_grad: float32 [1600], P('fsdp')
The draws below stay inside these ranges and needn't reach their ends.
Inputs may be any that keep to these rules, and one draw needn't show every extreme that they name: `doc_starts`: each row begins with 0 and rises strictly; document j of a sequence runs from its start to the next start. `pic_starts`: each row rises; the pieces of 256 positions never intersect and end within the sequence.
All inputs are finite; a program needn't handle non-finite values.
Results may differ from the reference program's by a relative error of at most 0.02.
Values may be sent and summed in bfloat16 or wider, within the bound.
No kernel may reach another device: no remote copies, remote signals or barrier semaphores. Data moves between devices by JAX's collectives and lax.ppermute only.
A program may use at most 320 MiB of HBM per device.

```python
import jax
import jax.numpy as jnp
from jax import lax

D = 1600
HEADS = 25
HD = 64
FF = 6400
PIECE = 256
SEQ = 1024
NSEQ = 4
TOKENS = 4096
PICS = 1


def draw_doc_starts(key, part):
    eighth = SEQ // 8
    key_one = jax.random.fold_in(key, 11)
    key_two = jax.random.fold_in(key, 23)
    second = 5 * eighth + jax.random.randint(key_one, (NSEQ, 1), 0, eighth)
    third = second + eighth + jax.random.randint(key_two, (NSEQ, 1), 0, eighth)
    first = jnp.zeros((NSEQ, 1), jnp.int32)
    return jnp.concatenate([first, second, third], axis=1).astype(jnp.int32)


def draw_pic_starts(key, part):
    slot_len = 2 * PIECE
    shifts = jax.random.randint(key, (NSEQ, PICS - 1), 0, PIECE + 1)
    offsets = jnp.arange(PICS - 1, dtype=jnp.int32) * slot_len
    early = (offsets[None, :] + shifts).astype(jnp.int32)
    last = jnp.full((NSEQ, 1), SEQ - PIECE, jnp.int32)
    return jnp.concatenate([early, last], axis=1).astype(jnp.int32)


def level_of(key, dims, split, least, largest):
    def one(axis_at, blocks):
        steps = jax.random.uniform(jax.random.fold_in(jax.random.fold_in(key, 6), axis_at), (blocks,), jnp.float32, least / len(split), largest / len(split))
        return jnp.repeat(jnp.exp(steps), dims[axis_at] // blocks).reshape((-1,) + (1,) * (len(dims) - axis_at - 1))

    level = one(*split[0])
    for cut in split[1:]:
        level = level * one(*cut)
    return level


def bell_draw(stream_key, dims, width, most, cuts=(), kind=jnp.bfloat16):
    entries = jax.random.normal(stream_key, dims, jnp.float32) * width
    if len(cuts) > 0:
        entries = level_of(stream_key, dims, cuts, -0.22, 0.18) * entries
    return jnp.clip(entries, min=-most, max=most).astype(kind)


def setup_inputs(seed: int = 0) -> dict:
    seeds = jax.random.split(jax.random.key(seed), 17)
    tokens = bell_draw(seeds[0], (TOKENS, D), 1.0, 6.0, ((0, 32),))
    doc_starts = draw_doc_starts(jax.random.fold_in(seeds[16], 71), 0)
    pic_starts = draw_pic_starts(jax.random.fold_in(seeds[16], 71), 0)
    ln1_gain = jnp.clip(1.0 + 0.18 * jax.random.normal(seeds[3], (D,), jnp.float32), 0.099609375, 1.8984375).astype(jnp.bfloat16)
    ln1_shift = bell_draw(seeds[4], (D,), 0.5, 3.0, ((0, 8),))
    w_qkv = bell_draw(seeds[5], (D, 3 * D), D ** -0.5, 0.15625, ((0, 8),))
    bias_qv = bell_draw(seeds[6], (2 * D,), 0.5, 3.0, ((0, 8),))
    w_attn = bell_draw(seeds[7], (D, D), (max(D // 256, 1)) ** -0.5, 2.5, ((0, 8),))
    bias_attn = bell_draw(seeds[8], (D,), 0.5, 3.0, ((0, 8),))
    ln2_gain = jnp.clip(1.0 + 0.18 * jax.random.normal(seeds[9], (D,), jnp.float32), 0.099609375, 1.8984375).astype(jnp.bfloat16)
    ln2_shift = bell_draw(seeds[10], (D,), 0.5, 3.0, ((0, 8),))
    w_fc = bell_draw(seeds[11], (D, FF), D ** -0.5, 0.15625, ((0, 8),))
    bias_fc = bell_draw(seeds[12], (FF,), 0.5, 3.0, ((0, 8),))
    w_proj = bell_draw(seeds[13], (FF, D), FF ** -0.5, 0.078125, ((0, 8),))
    bias_proj = bell_draw(seeds[14], (D,), 0.5, 3.0, ((0, 8),))
    cotangent = bell_draw(seeds[15], (TOKENS, D), 1.0, 6.0, ((0, 32),))
    return dict(tokens=tokens, doc_starts=doc_starts, pic_starts=pic_starts, ln1_gain=ln1_gain, ln1_shift=ln1_shift, w_qkv=w_qkv, bias_qv=bias_qv, w_attn=w_attn, bias_attn=bias_attn, ln2_gain=ln2_gain, ln2_shift=ln2_shift, w_fc=w_fc, bias_fc=bias_fc, w_proj=w_proj, bias_proj=bias_proj, cotangent=cotangent)


@jax.custom_vjp
def low(v):
    return lax.optimization_barrier(v.astype(jnp.bfloat16)).astype(jnp.float32)

@jax.custom_vjp
def low_back(v):
    return v

def low_keep(v):
    return (low(v), None)

def low_pass(kept, grad):
    return (grad,)

def back_keep(v):
    return (v, None)

def back_low(kept, grad):
    return (low(grad),)
low.defvjp(low_keep, low_pass)
low_back.defvjp(back_keep, back_low)
epsilon = 1e-05
neg_large = -1e+30
highest = lax.Precision.HIGHEST

def normalize(values, gain, shift):
    mean_v = lax.optimization_barrier(jnp.mean(values, axis=-1, keepdims=True))
    centred = values - mean_v
    variance = lax.optimization_barrier(jnp.mean(centred * centred, axis=-1, keepdims=True))
    return centred * lax.rsqrt(variance + epsilon) * gain + shift

def doc_index(positions, starts):
    return lax.optimization_barrier(jnp.sum((positions[:, None] >= starts[None, :]).astype(jnp.int32), axis=1))

def pic_index(positions, starts):
    inside = (positions[:, None] >= starts[None, :]) & (positions[:, None] < starts[None, :] + PIECE)
    labels = jnp.arange(1, starts.shape[0] + 1, dtype=jnp.int32)
    return lax.optimization_barrier(jnp.sum(jnp.where(inside, labels[None, :], 0), axis=1)) - 1

def allowed_pairs(query_pos, key_pos, doc_row, pic_row):
    same_doc = doc_index(query_pos, doc_row)[:, None] == doc_index(key_pos, doc_row)[None, :]
    causal = key_pos[None, :] <= query_pos[:, None]
    pic_query = pic_index(query_pos, pic_row)
    picture = (pic_query[:, None] == pic_index(key_pos, pic_row)[None, :]) & (pic_query[:, None] >= 0)
    return same_doc & (causal | picture)

def matmul(left, right):
    return jnp.dot(left, right, precision=highest, preferred_element_type=jnp.float32)

def layer(inputs, params, doc_row, pic_row):
    gain_one, shift_one, mat_qkv, bias_two, mat_attn, bias_out, gain_two, shift_two, mat_fc, bias_hidden, mat_proj, bias_last = params
    seq_len = inputs.shape[0]
    feat_dim = inputs.shape[1]
    normed_one = low(normalize(inputs, gain_one, shift_one))
    bias_full = jnp.concatenate([bias_two[:feat_dim], jnp.zeros((feat_dim,), jnp.float32), bias_two[feat_dim:]])
    qkv_vals = low(low_back(matmul(normed_one, mat_qkv) + bias_full))
    queries = qkv_vals[:, :feat_dim].reshape(seq_len, HEADS, HD)
    keys = qkv_vals[:, feat_dim:2 * feat_dim].reshape(seq_len, HEADS, HD)
    values = qkv_vals[:, 2 * feat_dim:].reshape(seq_len, HEADS, HD)
    positions = jnp.arange(seq_len, dtype=jnp.int32)
    block_len = min(512, seq_len)
    blocks = seq_len // block_len

    def one_block(item):
        query_blk, query_pos = item
        scores = jnp.einsum('qhd,khd->hqk', query_blk, keys, precision=highest) * HD ** (-0.5)
        scores = low_back(scores)
        allowed = allowed_pairs(query_pos, positions, doc_row, pic_row)
        scores = jnp.where(allowed[None], scores, neg_large)
        probs = low(jax.nn.softmax(scores, axis=-1))
        result = jnp.einsum('hqk,khd->qhd', probs, values, precision=highest)
        return result.reshape(query_blk.shape[0], feat_dim)
    attended = lax.map(jax.checkpoint(one_block), (queries.reshape(blocks, block_len, HEADS, HD), positions.reshape(blocks, block_len)))
    attended = low(low_back(attended.reshape(seq_len, feat_dim)))
    branch = low_back(matmul(attended, mat_attn) + bias_out)
    middle = inputs + branch
    normed_two = low(normalize(middle, gain_two, shift_two))
    hidden = low_back(matmul(normed_two, mat_fc) + bias_hidden)
    activ = low(jax.nn.gelu(hidden, approximate=True))
    return middle + matmul(activ, mat_proj) + bias_last

def reference(tokens, doc_starts, pic_starts, ln1_gain, ln1_shift, w_qkv, bias_qv, w_attn, bias_attn, ln2_gain, ln2_shift, w_fc, bias_fc, w_proj, bias_proj, cotangent):
    params = tuple((weight.astype(jnp.float32) for weight in (ln1_gain, ln1_shift, w_qkv, bias_qv, w_attn, bias_attn, ln2_gain, ln2_shift, w_fc, bias_fc, w_proj, bias_proj)))
    feat_dim = tokens.shape[1]
    inputs = tokens.astype(jnp.float32).reshape(NSEQ, SEQ, feat_dim)
    cots = cotangent.astype(jnp.float32).reshape(NSEQ, SEQ, feat_dim)
    zeros = tuple((jnp.zeros(weight.shape, jnp.float32) for weight in params))

    def step(totals, item):
        seq_in, seq_cot, doc_row, pic_row = item

        def forward(values, weights):
            return layer(values, weights, doc_row, pic_row)
        result, pull = jax.vjp(forward, seq_in, params)
        d_in, d_params = pull(seq_cot)
        totals = tuple((total + grad for total, grad in zip(totals, d_params)))
        return (totals, (result.astype(jnp.bfloat16), d_in.astype(jnp.bfloat16)))
    totals, (results, d_ins) = lax.scan(step, zeros, (inputs, cots, doc_starts, pic_starts))
    return (results.reshape(NSEQ * SEQ, feat_dim), d_ins.reshape(NSEQ * SEQ, feat_dim), totals[0], totals[1], totals[2], totals[3], totals[4], totals[5], totals[6], totals[7], totals[8], totals[9], totals[10], totals[11])
```

```python
import jax
import jax.numpy as jnp
from jax import lax
from jax.experimental import pallas as pl
from jax.experimental.pallas import tpu as pltpu
from jax.sharding import Mesh, PartitionSpec as P

HEADS = 25
HD = 64
PIECE = 256
SLOTS = 4


epsilon = 1e-05
neg_large = -1e30
F32 = jnp.float32
BF16 = jnp.bfloat16


def normalize(values, gain, shift):
    mean_v = jnp.mean(values, axis=-1, keepdims=True)
    centred = values - mean_v
    variance = jnp.mean(centred * centred, axis=-1, keepdims=True)
    return centred * lax.rsqrt(variance + epsilon) * gain + shift


def norm_plain(values, gain):
    return normalize(values, gain, 0.0)


def gelu_tanh(values):
    return jax.nn.gelu(values, approximate=True)


def mul(left, right):
    return jnp.dot(left, right, preferred_element_type=F32)


def cross(left, right):
    return lax.dot_general(left, right, (((0,), (0,)), ((), ())), preferred_element_type=F32)


def back_mul(left, weight):
    return lax.dot_general(left, weight, (((1,), (1,)), ((), ())), preferred_element_type=F32)


def flip(v, axis):
    return lax.ppermute(v, axis, [(0, 1), (1, 0)])


def z_flip(v, m):
    return lax.ppermute(v, "z", [(i, i ^ m) for i in range(4)])


def chip_flip(v, m):
    return lax.ppermute(v, ("y", "x"), [(i, i ^ m) for i in range(4)])


def swap_planes(v):
    return lax.ppermute(v, ("y", "x", "z"), [(4 * j + z, 4 * z + j) for j in range(4) for z in range(4)])


def in_order(parts, index):
    n = len(parts)
    return [lax.select_n(index, *[parts[k ^ m] for m in range(n)]) for k in range(n)]


def in_order2(own, other, index):
    first = index == 0
    return [jnp.where(first, own, other), jnp.where(first, other, own)]


def join_rows(parts):
    starts, total = [], 0
    for p in parts:
        starts.append(total)
        total += p.shape[0]

    def kernel(*refs):
        ins, out, sems = refs[: len(parts)], refs[len(parts)], refs[len(parts) + 1]
        copies = [
            pltpu.make_async_copy(r, out.at[pl.ds(at, p.shape[0]), :], sems.at[k])
            for k, (r, at, p) in enumerate(zip(ins, starts, parts))
        ]
        for copy in copies:
            copy.start()
        for copy in copies:
            copy.wait()

    return pl.pallas_call(
        kernel,
        out_shape=jax.ShapeDtypeStruct((total, parts[0].shape[1]), parts[0].dtype),
        in_specs=[pl.BlockSpec(memory_space=pl.ANY)] * len(parts),
        out_specs=pl.BlockSpec(memory_space=pltpu.VMEM),
        scratch_shapes=[pltpu.SemaphoreType.DMA((len(parts),))],
        name="join_rows",
    )(*parts)


def plane_gather(own):
    n = own.shape[0] // 2
    own_c = flip(own, "c")
    vx = flip(own, "x")
    vy = flip(own, "y")
    top = flip(vy[:n], "x")
    low = flip(vx[n:], "y")
    vx_c = flip(vx, "c")
    vy_c = flip(vy, "c")
    top_c = flip(top, "c")
    low_c = flip(low, "c")
    return join_rows([own, vx, vy, top, low, own_c, vx_c, vy_c, top_c, low_c])


def block_order(y, x, c):
    order = []
    for c_rel in range(2):
        for y_rel, x_rel in ((0, 0), (0, 1), (1, 0), (1, 1)):
            order.append(4 * (y ^ y_rel) + 2 * (x ^ x_rel) + (c ^ c_rel))
    return jnp.stack(order).astype(jnp.int32)


def add_low(left, right):
    return (left.astype(F32) + right.astype(F32)).astype(BF16)


def plane_scatter(part):
    n = part.shape[0] // 8
    k = n // 2
    h = add_low(part[: 4 * n], flip(part[4 * n :], "c"))
    own, vx, vy, far = h[:n], h[n : 2 * n], h[2 * n : 3 * n], h[3 * n :]
    top = flip(far[:k], "x")
    low = flip(far[k:], "y")
    vy = jnp.concatenate([add_low(vy[:k], top), vy[k:]])
    vx = jnp.concatenate([vx[:k], add_low(vx[k:], low)])
    return own.astype(F32) + flip(vx, "x").astype(F32) + flip(vy, "y").astype(F32)


def after(v, *deps):
    return lax.optimization_barrier((v,) + deps)[0]


def z_scatter(part, z):
    n = part.shape[0] // 4
    total = lax.dynamic_slice_in_dim(part, z * n, n, 0).astype(F32)
    for m in range(1, 4):
        piece = lax.dynamic_slice_in_dim(part, (z ^ m) * n, n, 0)
        total = total + z_flip(piece, m).astype(F32)
    return total.astype(BF16)


def small_sum(rows, z, core, chip, groups):
    v = rows.reshape(4, 2, -1)
    total = lax.dynamic_index_in_dim(v, z, 0, keepdims=False)
    for m in range(1, 4):
        total = total + z_flip(lax.dynamic_index_in_dim(v, z ^ m, 0, keepdims=False), m)
    mine = lax.dynamic_index_in_dim(total, core, 0, keepdims=False)
    theirs = lax.dynamic_index_in_dim(total, 1 - core, 0, keepdims=False)
    mine = mine + flip(theirs, "c")
    a, b, c, d = chips_gather(mine, chip)
    return group_sum((a + b) + (c + d), groups)


def group_sum(v, groups):
    return lax.psum(v, "g") if groups > 1 else v


def chips_gather(v, chip):
    return in_order([v] + [chip_flip(v, m) for m in range(1, 4)], chip)


def core_rows(v, core):
    n = v.shape[0] // 2
    mine = lax.dynamic_slice_in_dim(v, core * n, n, 0)
    theirs = lax.dynamic_slice_in_dim(v, (1 - core) * n, n, 0)
    return in_order2(mine, flip(theirs, "c"), core)


def reach(meta_ref, pos, docs, pics):
    first = jnp.zeros_like(pos)
    doc_end = jnp.full_like(pos, 1 << 20)
    for d in range(docs):
        start = meta_ref[8 + d]
        first = jnp.where(pos >= start, start, first)
    for d in range(docs - 1, -1, -1):
        start = meta_ref[8 + d]
        doc_end = jnp.where(pos < start, start, doc_end)
    last = pos
    for p in range(pics):
        start = meta_ref[8 + docs + p]
        inside = (pos >= start) & (pos < start + PIECE)
        last = jnp.where(inside, jnp.minimum(doc_end, start + PIECE) - 1, last)
    return first, last


def load_heads(meta_ref, qkv_ref, dest, third, seq, scale=None):
    run = seq // 8
    for t in range(8):
        place = pl.multiple_of(meta_ref[t] * run, run)
        vals = qkv_ref[t * run : (t + 1) * run, third * SLOTS * HD : (third + 1) * SLOTS * HD]
        if scale is not None:
            vals = (vals.astype(F32) * scale).astype(BF16)
        for h in range(SLOTS):
            dest[h, pl.ds(place, run), :] = vals[:, h * HD : (h + 1) * HD]


def attend(qkv, meta, docs, pics):
    seq = qkv.shape[0]
    blk = 256
    nb = seq // blk

    def kernel(meta_ref, qkv_ref, out_ref, rel_ref, lse_ref, q_s, k_s, v_s, o_s, l_s):
        load_heads(meta_ref, qkv_ref, q_s, 0, seq, HD**-0.5)
        load_heads(meta_ref, qkv_ref, k_s, 1, seq)
        load_heads(meta_ref, qkv_ref, v_s, 2, seq)

        def head(h, carry):
            for i in range(nb):
                span = min(seq, (i + 2) * blk)
                pos = i * blk + lax.broadcasted_iota(jnp.int32, (blk, 1), 0)
                first, last = reach(meta_ref, pos, docs, pics)
                key = lax.broadcasted_iota(jnp.int32, (blk, span), 1)
                s = back_mul(q_s[h, i * blk : (i + 1) * blk, :], k_s[h, 0:span, :])
                s = jnp.where((key >= first) & (key <= last), s, neg_large)
                top = jnp.max(s, axis=1, keepdims=True)
                e = jnp.exp(s - top)
                total = jnp.sum(e, axis=1, keepdims=True)
                probs = (e * (1.0 / total)).astype(BF16)
                o_s[h, i * blk : (i + 1) * blk, :] = mul(probs, v_s[h, 0:span, :]).astype(BF16)
                l_s[h, i * blk : (i + 1) * blk, :] = top + jnp.log(total)
            return carry

        lax.fori_loop(0, SLOTS, head, 0)
        for h in range(SLOTS):
            out_ref[:, h * HD : (h + 1) * HD] = o_s[h]
            lse_ref[:, h : h + 1] = l_s[h]
            for t in range(8):
                place = pl.multiple_of(meta_ref[t] * (seq // 8), seq // 8)
                rel_ref[t * (seq // 8) : (t + 1) * (seq // 8), h * HD : (h + 1) * HD] = o_s[h, pl.ds(place, seq // 8), :]

    return pl.pallas_call(
        kernel,
        out_shape=(
            jax.ShapeDtypeStruct((seq, SLOTS * HD), BF16),
            jax.ShapeDtypeStruct((seq, SLOTS * HD), BF16),
            jax.ShapeDtypeStruct((seq, SLOTS), F32),
        ),
        in_specs=[
            pl.BlockSpec(memory_space=pltpu.SMEM),
            pl.BlockSpec(memory_space=pltpu.VMEM),
        ],
        out_specs=(
            pl.BlockSpec(memory_space=pltpu.VMEM),
            pl.BlockSpec(memory_space=pltpu.VMEM),
            pl.BlockSpec(memory_space=pltpu.VMEM),
        ),
        scratch_shapes=[pltpu.VMEM((SLOTS, seq, HD), BF16)] * 4
        + [pltpu.VMEM((SLOTS, seq, 1), F32)],
        name="attend",
    )(meta, qkv)


def attend_back(qkv, att, d_att, lse, meta, docs, pics):
    seq = qkv.shape[0]
    blk = 256
    nb = seq // blk
    scale = HD**-0.5

    def kernel(meta_ref, qkv_ref, att_ref, datt_ref, lse_ref, out_ref, q_s, k_s, v_s, d_s, dq_s, dk_s, dv_s, delta_s):
        load_heads(meta_ref, qkv_ref, q_s, 0, seq, scale)
        load_heads(meta_ref, qkv_ref, k_s, 1, seq)
        load_heads(meta_ref, qkv_ref, v_s, 2, seq)
        ones = jnp.ones((8, HD), F32)
        for h in range(SLOTS):
            cols = slice(h * HD, (h + 1) * HD)
            d_s[h] = datt_ref[:, cols]
            prod = datt_ref[:, cols].astype(F32) * att_ref[:, cols].astype(F32)
            delta_s[h] = lax.dot_general(
                ones, prod, (((1,), (1,)), ((), ())), precision=lax.Precision.HIGHEST,
                preferred_element_type=F32,
            )[0:1]
        pos = lax.broadcasted_iota(jnp.int32, (1, seq), 1)
        first, last = reach(meta_ref, pos, docs, pics)

        def head(h, carry):
            dq_s[h] = jnp.zeros((seq, HD), F32)
            lse_h = lse_ref[h]
            for i in range(nb):
                low = max(0, i - 1) * blk
                rows = slice(i * blk, (i + 1) * blk)
                k_b = k_s[h, rows, :]
                q_b = q_s[h, low:, :]
                d_b = d_s[h, low:, :]
                s = back_mul(k_b, q_b)
                key = i * blk + lax.broadcasted_iota(jnp.int32, s.shape, 0)
                ok = (key >= first[:, low:]) & (key <= last[:, low:])
                p = jnp.where(ok, jnp.exp(s - lse_h[:, low:]), 0.0)
                dp = back_mul(v_s[h, rows, :], d_b)
                ds = (p * (dp - delta_s[h, :, low:])).astype(BF16)
                dv_s[h, rows, :] = mul(p.astype(BF16), d_b).astype(BF16)
                dk_s[h, rows, :] = mul(ds, q_b).astype(BF16)
                dq_s[h, low:, :] += cross(ds, k_b)
            return carry

        lax.fori_loop(0, SLOTS, head, 0)
        run = seq // 8
        for t in range(8):
            place = pl.multiple_of(meta_ref[t] * run, run)
            dst = slice(t * run, (t + 1) * run)
            for h in range(SLOTS):
                out_ref[dst, h * HD : (h + 1) * HD] = (dq_s[h, pl.ds(place, run), :] * scale).astype(BF16)
                out_ref[dst, (SLOTS + h) * HD : (SLOTS + h + 1) * HD] = dk_s[h, pl.ds(place, run), :]
                out_ref[dst, (2 * SLOTS + h) * HD : (2 * SLOTS + h + 1) * HD] = dv_s[h, pl.ds(place, run), :]

    vmem = pl.BlockSpec(memory_space=pltpu.VMEM)
    return pl.pallas_call(
        kernel,
        out_shape=jax.ShapeDtypeStruct((seq, 3 * SLOTS * HD), BF16),
        in_specs=[pl.BlockSpec(memory_space=pltpu.SMEM), vmem, vmem, vmem, vmem],
        out_specs=vmem,
        scratch_shapes=[pltpu.VMEM((SLOTS, seq, HD), BF16)] * 4
        + [pltpu.VMEM((SLOTS, seq, HD), F32)]
        + [pltpu.VMEM((SLOTS, seq, HD), BF16)] * 2
        + [pltpu.VMEM((SLOTS, 1, seq), F32)],
        name="attend_back",
    )(meta, qkv, att, d_att, lse)


def on_device(groups):
    def run(tokens, doc_starts, pic_starts, ln1_gain, ln1_shift, w_qkv, bias_qv, w_attn, bias_attn,
            ln2_gain, ln2_shift, w_fc, bias_fc, w_proj, bias_proj, cotangent):
        y = lax.axis_index("y")
        x = lax.axis_index("x")
        z = lax.axis_index("z")
        c = lax.axis_index("c")
        chip = 2 * y + x
        rows, feat = tokens.shape
        docs, pics = doc_starts.shape[1], pic_starts.shape[1]
        ff = w_fc.shape[1]
        wrows = w_qkv.shape[0]
        hid = ff // 8
        sub = hid // 4
        width = SLOTS * HD
        last_start = feat - 2 * width
        chip_col = jnp.minimum(2 * width * chip, last_start)
        core_col = chip_col + width * c
        real = feat - 6 * width

        vec = jnp.concatenate([ln1_gain, ln1_shift, bias_qv, bias_attn, ln2_gain, ln2_shift, bias_fc, bias_proj])

        def head_columns(start):
            return jnp.concatenate(
                [lax.dynamic_slice_in_dim(w_qkv, k * feat + start, width, 1) for k in range(3)], axis=1
            )
        mine = head_columns(core_col)
        theirs = head_columns(chip_col + width * (1 - c))
        qkv_rows = jnp.concatenate(in_order2(mine, flip(theirs, "c"), c))
        mat_qkv = lax.all_gather(qkv_rows, "z", axis=0, tiled=True)

        tok = swap_planes(tokens)
        vec = jnp.stack(in_order2(vec, flip(vec, "c"), c))
        vecs = jnp.stack(in_order([vec] + [z_flip(vec, m) for m in range(1, 4)], z)).reshape(8, -1)
        numbers = swap_planes(jnp.concatenate([doc_starts[0], pic_starts[0]]))

        step = feat // 4 // 128 * 128
        window = feat - 3 * step
        attn_cols = lax.dynamic_slice_in_dim(w_attn, step * chip, window, 1)
        attn_z = jnp.concatenate(in_order([attn_cols] + [z_flip(attn_cols, m) for m in range(1, 4)], z))

        def hidden_columns(core):
            return jnp.concatenate(
                [lax.dynamic_slice_in_dim(w_fc, hid * (2 * k + core) + sub * chip, sub, 1) for k in range(4)], axis=1
            )
        fc_rows = jnp.concatenate(in_order2(hidden_columns(c), flip(hidden_columns(1 - c), "c"), c))
        mat_fc = lax.all_gather(fc_rows, "z", axis=0, tiled=True)
        proj_rows = lax.dynamic_slice_in_dim(w_proj, sub * chip, sub, 0)
        mat_proj = lax.all_gather(proj_rows, "z", axis=0, tiled=True)

        def take(start, size):
            return vecs[:, start : start + size].astype(F32)
        gain_one = take(0, wrows).reshape(-1)
        shift_one = take(wrows, wrows).reshape(-1)
        bias_two = take(2 * wrows, 2 * wrows).reshape(2, feat)
        bias_out = take(4 * wrows, wrows).reshape(-1)
        gain_two = take(5 * wrows, wrows).reshape(-1)
        shift_two = take(6 * wrows, wrows).reshape(-1)
        bias_hidden = take(7 * wrows, hid).reshape(4, 2, 4, sub)
        bias_hidden = lax.dynamic_slice(bias_hidden, (0, c, chip, 0), (4, 1, 1, sub)).reshape(hid)
        bias_last = take(7 * wrows + hid, wrows).reshape(-1)
        bias_heads = lax.dynamic_slice(bias_two, (0, core_col), (2, width))
        bias_full = jnp.concatenate([bias_heads[0], jnp.zeros((width,), F32), bias_heads[1]])

        meta = jnp.concatenate([block_order(y, x, c), numbers])
        inputs = tok.astype(F32)
        normed_one = plane_gather(normalize(inputs, gain_one, shift_one).astype(BF16))
        attn_z = after(attn_z, normed_one)
        attn_parts = chips_gather(attn_z, chip)
        attn_mine = jnp.concatenate([p[:, :step] for p in attn_parts[:3]] + [attn_parts[3]], axis=1)
        attn_theirs = flip(attn_mine, "c")
        cot_own = swap_planes(after(cotangent, normed_one))
        qkv = (mul(normed_one, mat_qkv) + bias_full).astype(BF16)
        att, att_rel, lse = attend(qkv, meta, docs, pics)
        att_rows = lax.all_to_all(att, ("y", "x", "c"), 0, 0, tiled=True).reshape(8, rows, width)
        att_own = jnp.concatenate(
            [att_rows[k] for k in range(6)] + [att_rows[7][:, width - real :]], axis=1
        )
        att_split = att_own.reshape(rows, 4, 2, wrows)
        att_even = att_split[:, :, 0].reshape(rows, feat // 2)
        att_odd = att_split[:, :, 1].reshape(rows, feat // 2)
        att_mine = jnp.where(c == 0, att_even, att_odd)
        att_theirs = jnp.where(c == 0, att_odd, att_even)
        middle = inputs + (mul(att_mine, attn_mine) + mul(att_theirs, attn_theirs)) + bias_out

        normed_two = plane_gather(normalize(middle, gain_two, shift_two).astype(BF16))
        cot = plane_gather(cot_own)
        hidden = mul(normed_two, mat_fc) + bias_hidden
        activ = gelu_tanh(hidden).astype(BF16)

        grad_in = cot_own.astype(F32)
        d_activ = back_mul(cot, mat_proj)
        unused_value, gelu_pull = jax.vjp(gelu_tanh, hidden)
        d_hidden = gelu_pull(d_activ)[0].astype(BF16)
        g_bias_hidden = jnp.sum(d_hidden.astype(F32), axis=0)
        d_normed_two = plane_scatter(back_mul(d_hidden, mat_fc).astype(BF16))
        g_proj = cross(activ, cot).astype(BF16)
        g_fc = cross(normed_two, d_hidden).astype(BF16)
        g_proj = group_sum(lax.psum_scatter(g_proj, "z", scatter_dimension=0, tiled=True), groups)
        g_fc = group_sum(lax.psum_scatter(g_fc, "z", scatter_dimension=0, tiled=True), groups)

        unused_two, pull_two = jax.vjp(norm_plain, middle, gain_two)
        d_mid_norm, g_gain_two = pull_two(d_normed_two)
        g_shift_two = jnp.sum(d_normed_two, axis=0)
        d_middle = grad_in + d_mid_norm
        d_branch = d_middle.astype(BF16)
        g_bias_out = jnp.sum(d_branch.astype(F32), axis=0)

        d_mine = back_mul(d_branch, attn_mine).astype(BF16)
        d_theirs = back_mul(d_branch, attn_theirs).astype(BF16)
        d_even = jnp.where(c == 0, d_mine, d_theirs).reshape(rows, 4, 1, wrows)
        d_odd = jnp.where(c == 0, d_theirs, d_mine).reshape(rows, 4, 1, wrows)
        d_own = jnp.concatenate([d_even, d_odd], axis=2).reshape(rows, feat)
        d_rows = jnp.concatenate(
            [d_own[:, k * width : (k + 1) * width] for k in range(6)]
            + [jnp.zeros((rows, width), BF16)]
            + [jnp.concatenate([jnp.zeros((rows, width - real), BF16), d_own[:, 6 * width :]], axis=1)]
        )
        d_att = lax.all_to_all(d_rows, ("y", "x", "c"), 0, 0, tiled=True)
        lse_rows = jnp.transpose(lse)[:, None, :]
        d_qkv = attend_back(qkv, att, d_att, lse_rows, meta, docs, pics)
        d_normed_one = plane_scatter(back_mul(d_qkv, mat_qkv).astype(BF16))

        g_qkv = cross(normed_one, d_qkv).astype(BF16)
        g_qkv = group_sum(z_scatter(g_qkv, z), groups)
        branch_all = plane_gather(after(d_branch, d_rows))
        g_heads = cross(att_rel, branch_all).astype(BF16)
        eighth = feat // 8
        g_heads = jnp.transpose(g_heads.reshape(width, 8, eighth), (1, 0, 2)).reshape(8 * width, eighth)
        g_heads = lax.all_to_all(g_heads, ("y", "x", "c"), 0, 0, tiled=True)
        g_attn = jnp.concatenate([g_heads[: 6 * width], g_heads[8 * width - real :]])
        g_attn = group_sum(z_scatter(g_attn, z), groups)

        out_own = middle + plane_scatter(mul(activ, mat_proj).astype(BF16)) + bias_last
        output = swap_planes(out_own.astype(BF16))

        unused_one, pull_one = jax.vjp(norm_plain, inputs, gain_one)
        d_in_norm, g_gain_one = pull_one(d_normed_one)
        g_shift_one = jnp.sum(d_normed_one, axis=0)
        tokens_grad = swap_planes((d_middle + d_in_norm).astype(BF16))

        proj_parts = chips_gather(g_proj, chip)
        w_proj_grad = jnp.concatenate(proj_parts).astype(F32)
        fc_parts = chips_gather(jnp.concatenate(core_rows(g_fc, c)), chip)
        w_fc_grad = jnp.concatenate(
            [
                fc_parts[at][core * wrows : (core + 1) * wrows, k * sub : (k + 1) * sub]
                for k in range(4) for core in range(2) for at in range(4)
            ],
            axis=1,
        ).astype(F32)
        attn_grads = chips_gather(jnp.concatenate(core_rows(g_attn, c), axis=1), chip)
        w_attn_grad = jnp.concatenate(attn_grads, axis=1).astype(F32)
        qkv_parts = chips_gather(jnp.concatenate(core_rows(g_qkv, c)), chip)
        columns = []
        for k in range(3):
            for chip_at in range(3):
                for core_at in range(2):
                    columns.append(qkv_parts[chip_at][core_at * wrows : (core_at + 1) * wrows, k * width : (k + 1) * width])
            columns.append(qkv_parts[3][wrows:, (k + 1) * width - real : (k + 1) * width])
        w_qkv_grad = jnp.concatenate(columns, axis=1).astype(F32)

        def by_row(*vectors):
            return [v.reshape(8, wrows) for v in vectors]
        hidden_slot = lax.dynamic_update_slice(
            jnp.zeros((4, 2, 4, sub), F32), g_bias_hidden.reshape(4, 1, 1, sub), (0, c, chip, 0)
        ).reshape(8, hid)
        g_bias_last = jnp.sum(grad_in, axis=0)
        early = small_sum(
            jnp.concatenate(by_row(g_bias_out, g_gain_two, g_shift_two, g_bias_last) + [hidden_slot], axis=1),
            z, c, chip, groups,
        )
        d_qkv_sums = jnp.sum(d_qkv.astype(F32), axis=0)
        heads_slot = lax.dynamic_update_slice(
            jnp.zeros((2, feat), F32),
            jnp.stack([d_qkv_sums[:width], d_qkv_sums[2 * width :]]),
            (0, core_col),
        ).reshape(8, 2 * wrows)
        late = small_sum(
            jnp.concatenate(by_row(g_gain_one, g_shift_one) + [heads_slot], axis=1), z, c, chip, groups
        )
        e = [early[k * wrows : (k + 1) * wrows] for k in range(4)]

        return (
            output, tokens_grad, late[:wrows], late[wrows : 2 * wrows], w_qkv_grad, late[2 * wrows :], w_attn_grad,
            e[0], e[1], e[2], w_fc_grad, early[4 * wrows :], w_proj_grad, e[3],
        )

    return run


def solution(mesh):
    reps = mesh.shape["rep"]
    line = mesh.shape["fsdp"]
    if reps % 4 or line != 8:
        raise ValueError("mesh")
    groups = reps // 4
    fine = Mesh(mesh.devices.reshape(groups, 2, 2, line // 2, 2), ("g", "y", "x", "z", "c"))
    every = ("g", "y", "x", "z", "c")
    rep = ("g", "y", "x")
    shard = ("z", "c")
    vec, mat, rowed = P(shard), P(shard, None), P(every, None)
    placed = (rowed, P(rep, None), P(rep, None), vec, vec, mat, vec, mat, vec, vec, vec, mat, vec, mat, vec, rowed)
    outs = (rowed, rowed, vec, vec, mat, vec, mat, vec, vec, vec, mat, vec, mat, vec)
    return jax.shard_map(on_device(groups), mesh=fine, in_specs=placed, out_specs=outs, check_vma=False)
```

```python
import jax
import jax.numpy as jnp
from jax import lax
from jax.experimental import pallas as pl
from jax.experimental.pallas import tpu as pltpu
from jax.sharding import Mesh, PartitionSpec as P

HD = 64
PIECE = 256
SLOTS = 4


epsilon = 1e-05
neg_large = -1e30
F32 = jnp.float32
BF16 = jnp.bfloat16


def normalize(values, gain, shift):
    mean_v = jnp.mean(values, axis=-1, keepdims=True)
    centred = values - mean_v
    variance = jnp.mean(centred * centred, axis=-1, keepdims=True)
    return centred * lax.rsqrt(variance + epsilon) * gain + shift


def norm_plain(values, gain):
    return normalize(values, gain, 0.0)


def gelu_tanh(values):
    return jax.nn.gelu(values, approximate=True)


def mul(left, right):
    return jnp.dot(left, right, preferred_element_type=F32)


def cross(left, right):
    return lax.dot_general(left, right, (((0,), (0,)), ((), ())), preferred_element_type=F32)


def back_mul(left, weight):
    return lax.dot_general(left, weight, (((1,), (1,)), ((), ())), preferred_element_type=F32)


def flip(v, axis):
    return lax.ppermute(v, axis, [(0, 1), (1, 0)])


def z_flip(v, m):
    return lax.ppermute(v, "z", [(i, i ^ m) for i in range(4)])


def chip_flip(v, m):
    return lax.ppermute(v, ("y", "x"), [(i, i ^ m) for i in range(4)])


def swap_planes(v):
    return lax.ppermute(v, ("y", "x", "z"), [(4 * j + z, 4 * z + j) for j in range(4) for z in range(4)])


def in_order(parts, index):
    n = len(parts)
    return [lax.select_n(index, *[parts[k ^ m] for m in range(n)]) for k in range(n)]


def in_order2(own, other, index):
    first = index == 0
    return [jnp.where(first, own, other), jnp.where(first, other, own)]


def join_rows(parts):
    starts, total = [], 0
    for p in parts:
        starts.append(total)
        total += p.shape[0]

    def kernel(*refs):
        ins, out, sems = refs[: len(parts)], refs[len(parts)], refs[len(parts) + 1]
        copies = [
            pltpu.make_async_copy(r, out.at[pl.ds(at, p.shape[0]), :], sems.at[k])
            for k, (r, at, p) in enumerate(zip(ins, starts, parts))
        ]
        for copy in copies:
            copy.start()
        for copy in copies:
            copy.wait()

    return pl.pallas_call(
        kernel,
        out_shape=jax.ShapeDtypeStruct((total, parts[0].shape[1]), parts[0].dtype),
        in_specs=[pl.BlockSpec(memory_space=pl.ANY)] * len(parts),
        out_specs=pl.BlockSpec(memory_space=pltpu.VMEM),
        scratch_shapes=[pltpu.SemaphoreType.DMA((len(parts),))],
        name="join_rows",
    )(*parts)


def join_columns(parts, chip, step):
    height, window = parts[0].shape
    total = 3 * step + window

    def kernel(chip_ref, *refs):
        out = refs[4]
        for m in range(4):
            place = chip_ref[0] ^ m
            out[:, pl.ds(pl.multiple_of(place * step, 128), step)] = refs[m][:, :step]

            @pl.when(place == 3)
            def _():
                out[:, 4 * step :] = refs[m][:, step:]

    vmem = pl.BlockSpec(memory_space=pltpu.VMEM)
    return pl.pallas_call(
        kernel,
        out_shape=jax.ShapeDtypeStruct((height, total), parts[0].dtype),
        in_specs=[pl.BlockSpec(memory_space=pltpu.SMEM)] + [vmem] * 4,
        out_specs=vmem,
        name="join_columns",
    )(chip.reshape(1).astype(jnp.int32), *parts)


def gather_first(own):
    return own, flip(own, "c"), flip(own, "x"), flip(own, "y")


def gather_second(first):
    own, own_c, vx, vy = first
    n = own.shape[0] // 2
    top = flip(vy[:n], "x")
    low = flip(vx[n:], "y")
    return [own, vx, vy, top, low, own_c, flip(vx, "c"), flip(vy, "c"), flip(top, "c"), flip(low, "c")]


def block_order(y, x, c):
    order = []
    for c_rel in range(2):
        for y_rel, x_rel in ((0, 0), (0, 1), (1, 0), (1, 1)):
            order.append(4 * (y ^ y_rel) + 2 * (x ^ x_rel) + (c ^ c_rel))
    return jnp.stack(order).astype(jnp.int32)


def vmem_call(kernel, shapes, scalar, operands):
    vmem = pl.BlockSpec(memory_space=pltpu.VMEM)
    return pl.pallas_call(
        kernel,
        out_shape=tuple(jax.ShapeDtypeStruct(dims, kind) for dims, kind in shapes),
        in_specs=[pl.BlockSpec(memory_space=pltpu.SMEM)] + [vmem] * len(operands),
        out_specs=(vmem,) * len(shapes),
    )(scalar.reshape(1).astype(jnp.int32), *operands)


def scatter_first(near, far, core):
    got = flip(far, "c")
    n = near.shape[0] // 4
    k = n // 2
    cols = near.shape[1]

    def kernel(core_ref, near_ref, got_ref, own_ref, x_ref, y_ref, top_ref, low_ref):
        at = 0
        for ref in (own_ref, x_ref, y_ref, top_ref, low_ref):
            run = slice(at, at + ref.shape[0])
            ref[...] = (near_ref[run, :].astype(F32) + got_ref[run, :].astype(F32)).astype(BF16)
            at += ref.shape[0]

    shapes = [((rows, cols), BF16) for rows in (n, n, n, k, k)]
    own, vx, vy, top, low = vmem_call(kernel, shapes, core, [near, got])
    return own, vx, vy, flip(top, "x"), flip(low, "y")


def scatter_second(first, core):
    own, vx, vy, top, low = first
    k = top.shape[0]

    def kernel(core_ref, x_ref, y_ref, top_ref, low_ref, x_out, y_out):
        x_out[:k, :] = x_ref[:k, :]
        x_out[k:, :] = (x_ref[k:, :].astype(F32) + low_ref[...].astype(F32)).astype(BF16)
        y_out[:k, :] = (y_ref[:k, :].astype(F32) + top_ref[...].astype(F32)).astype(BF16)
        y_out[k:, :] = y_ref[k:, :]

    vx, vy = vmem_call(kernel, [(vx.shape, BF16)] * 2, core, [vx, vy, top, low])
    return own, flip(vx, "x"), flip(vy, "y")


def scatter_sum(second):
    own, vx, vy = second
    return own.astype(F32) + vx.astype(F32) + vy.astype(F32)


def halves(left, right, product):
    n = left.shape[0] // 2
    far = product(left[n:], right).astype(BF16)
    near = product(left[:n], right).astype(BF16)
    return near, far


def assemble(parts, chip, shape, pieces):
    def kernel(chip_ref, *refs):
        out = refs[4]
        here = chip_ref[0]
        for row, col, at, from_row, rows, from_col, cols in pieces:
            take = (slice(from_row, from_row + rows), slice(from_col, from_col + cols))
            val = refs[0][take].astype(F32)
            for m in range(1, 4):
                val = jnp.where(here == (at ^ m), refs[m][take].astype(F32), val)
            out[row : row + rows, col : col + cols] = val

    return vmem_call(kernel, [(shape, F32)], chip, parts)[0]


def after(v, *deps):
    return lax.optimization_barrier((v, deps))[0]


def z_scatter_parts(part, z):
    n = part.shape[0] // 4
    parts = [lax.dynamic_slice_in_dim(part, z * n, n, 0)]
    for m in range(1, 4):
        parts.append(z_flip(lax.dynamic_slice_in_dim(part, (z ^ m) * n, n, 0), m))
    return parts


def core_rows(parts, core, groups):
    n = parts[0].shape[0] // 2
    cols = parts[0].shape[1]

    def sum_kernel(core_ref, *refs):
        mine_ref, theirs_ref = refs[-2:]

        def total(run):
            vals = [r[run, :].astype(F32) for r in refs[:-2]]
            while len(vals) > 1:
                vals = [vals[k] + vals[k + 1] for k in range(0, len(vals), 2)]
            return vals[0].astype(BF16)

        low, high = total(slice(0, n)), total(slice(n, 2 * n))
        first = core_ref[0] == 0
        mine_ref[...] = jnp.where(first, low, high)
        theirs_ref[...] = jnp.where(first, high, low)

    mine, theirs = vmem_call(sum_kernel, [((n, cols), BF16)] * 2, core, parts)
    got = flip(group_sum(theirs, groups), "c")
    mine = group_sum(mine, groups)

    def stack_kernel(core_ref, mine_ref, got_ref, out_ref):
        first = core_ref[0] == 0
        out_ref[:n, :] = jnp.where(first, mine_ref[...], got_ref[...])
        out_ref[n:, :] = jnp.where(first, got_ref[...], mine_ref[...])

    return vmem_call(stack_kernel, [((2 * n, cols), BF16)], core, [mine, got])[0]


def chip_parts(v):
    return [v] + [chip_flip(v, m) for m in range(1, 4)]


def small_sum(rows, z, core, chip, groups):
    v = rows.reshape(4, 2, -1)
    total = lax.dynamic_index_in_dim(v, z, 0, keepdims=False)
    for m in range(1, 4):
        total = total + z_flip(lax.dynamic_index_in_dim(v, z ^ m, 0, keepdims=False), m)
    mine = lax.dynamic_index_in_dim(total, core, 0, keepdims=False)
    theirs = lax.dynamic_index_in_dim(total, 1 - core, 0, keepdims=False)
    mine = mine + flip(theirs, "c")
    a, b, c, d = chips_gather(mine, chip)
    return group_sum((a + b) + (c + d), groups)


def group_sum(v, groups):
    return lax.psum(v, "g") if groups > 1 else v


def chips_gather(v, chip):
    return in_order([v] + [chip_flip(v, m) for m in range(1, 4)], chip)


def reach(meta_ref, pos, docs, pics):
    first = jnp.zeros_like(pos)
    doc_end = jnp.full_like(pos, 1 << 20)
    for d in range(docs):
        start = meta_ref[8 + d]
        first = jnp.where(pos >= start, start, first)
    for d in range(docs - 1, -1, -1):
        start = meta_ref[8 + d]
        doc_end = jnp.where(pos < start, start, doc_end)
    last = pos
    for p in range(pics):
        start = meta_ref[8 + docs + p]
        inside = (pos >= start) & (pos < start + PIECE)
        last = jnp.where(inside, jnp.minimum(doc_end, start + PIECE) - 1, last)
    return first, last


def load_heads(meta_ref, qkv_ref, dest, third, seq, scale=None):
    run = seq // 8
    for t in range(8):
        place = pl.multiple_of(meta_ref[t] * run, run)
        vals = qkv_ref[t * run : (t + 1) * run, third * SLOTS * HD : (third + 1) * SLOTS * HD]
        if scale is not None:
            vals = (vals.astype(F32) * scale).astype(BF16)
        for h in range(SLOTS):
            dest[h, pl.ds(place, run), :] = vals[:, h * HD : (h + 1) * HD]


def attend(qkv, meta, docs, pics):
    seq = qkv.shape[0]
    blk = 256
    nb = seq // blk

    def kernel(meta_ref, qkv_ref, out_ref, rel_ref, lse_ref, q_s, k_s, v_s, o_s, l_s):
        load_heads(meta_ref, qkv_ref, q_s, 0, seq, HD**-0.5)
        load_heads(meta_ref, qkv_ref, k_s, 1, seq)
        load_heads(meta_ref, qkv_ref, v_s, 2, seq)

        def head(h, carry):
            for i in range(nb):
                span = min(seq, (i + 2) * blk)
                pos = i * blk + lax.broadcasted_iota(jnp.int32, (blk, 1), 0)
                first, last = reach(meta_ref, pos, docs, pics)
                key = lax.broadcasted_iota(jnp.int32, (blk, span), 1)
                s = back_mul(q_s[h, i * blk : (i + 1) * blk, :], k_s[h, 0:span, :])
                s = jnp.where((key >= first) & (key <= last), s, neg_large)
                top = jnp.max(s, axis=1, keepdims=True)
                e = jnp.exp(s - top)
                total = jnp.sum(e, axis=1, keepdims=True)
                probs = (e * (1.0 / total)).astype(BF16)
                o_s[h, i * blk : (i + 1) * blk, :] = mul(probs, v_s[h, 0:span, :]).astype(BF16)
                l_s[h, i * blk : (i + 1) * blk, :] = top + jnp.log(total)
            return carry

        lax.fori_loop(0, SLOTS, head, 0)
        for h in range(SLOTS):
            out_ref[:, h * HD : (h + 1) * HD] = o_s[h]
            lse_ref[:, h : h + 1] = l_s[h]
            for t in range(8):
                place = pl.multiple_of(meta_ref[t] * (seq // 8), seq // 8)
                rel_ref[t * (seq // 8) : (t + 1) * (seq // 8), h * HD : (h + 1) * HD] = o_s[h, pl.ds(place, seq // 8), :]

    return pl.pallas_call(
        kernel,
        out_shape=(
            jax.ShapeDtypeStruct((seq, SLOTS * HD), BF16),
            jax.ShapeDtypeStruct((seq, SLOTS * HD), BF16),
            jax.ShapeDtypeStruct((seq, SLOTS), F32),
        ),
        in_specs=[
            pl.BlockSpec(memory_space=pltpu.SMEM),
            pl.BlockSpec(memory_space=pltpu.VMEM),
        ],
        out_specs=(
            pl.BlockSpec(memory_space=pltpu.VMEM),
            pl.BlockSpec(memory_space=pltpu.VMEM),
            pl.BlockSpec(memory_space=pltpu.VMEM),
        ),
        scratch_shapes=[pltpu.VMEM((SLOTS, seq, HD), BF16)] * 4
        + [pltpu.VMEM((SLOTS, seq, 1), F32)],
        name="attend",
    )(meta, qkv)


def attend_back(qkv, att, d_att, lse, meta, docs, pics):
    seq = qkv.shape[0]
    blk = 256
    nb = seq // blk
    scale = HD**-0.5

    def kernel(meta_ref, qkv_ref, att_ref, datt_ref, lse_ref, out_ref, q_s, k_s, v_s, d_s, dq_s, dk_s, dv_s, delta_s):
        load_heads(meta_ref, qkv_ref, q_s, 0, seq, scale)
        load_heads(meta_ref, qkv_ref, k_s, 1, seq)
        load_heads(meta_ref, qkv_ref, v_s, 2, seq)
        ones = jnp.ones((8, HD), F32)
        for h in range(SLOTS):
            cols = slice(h * HD, (h + 1) * HD)
            d_s[h] = datt_ref[:, cols]
            prod = datt_ref[:, cols].astype(F32) * att_ref[:, cols].astype(F32)
            delta_s[h] = lax.dot_general(
                ones, prod, (((1,), (1,)), ((), ())), precision=lax.Precision.HIGHEST,
                preferred_element_type=F32,
            )[0:1]
        pos = lax.broadcasted_iota(jnp.int32, (1, seq), 1)
        first, last = reach(meta_ref, pos, docs, pics)

        def head(h, carry):
            dq_s[h] = jnp.zeros((seq, HD), F32)
            lse_h = lse_ref[h]
            for i in range(nb):
                low = max(0, i - 1) * blk
                rows = slice(i * blk, (i + 1) * blk)
                k_b = k_s[h, rows, :]
                q_b = q_s[h, low:, :]
                d_b = d_s[h, low:, :]
                s = back_mul(k_b, q_b)
                key = i * blk + lax.broadcasted_iota(jnp.int32, s.shape, 0)
                ok = (key >= first[:, low:]) & (key <= last[:, low:])
                p = jnp.where(ok, jnp.exp(s - lse_h[:, low:]), 0.0)
                dp = back_mul(v_s[h, rows, :], d_b)
                ds = (p * (dp - delta_s[h, :, low:])).astype(BF16)
                dv_s[h, rows, :] = mul(p.astype(BF16), d_b).astype(BF16)
                dk_s[h, rows, :] = mul(ds, q_b).astype(BF16)
                dq_s[h, low:, :] += cross(ds, k_b)
            return carry

        lax.fori_loop(0, SLOTS, head, 0)
        run = seq // 8
        for t in range(8):
            place = pl.multiple_of(meta_ref[t] * run, run)
            dst = slice(t * run, (t + 1) * run)
            for h in range(SLOTS):
                out_ref[dst, h * HD : (h + 1) * HD] = (dq_s[h, pl.ds(place, run), :] * scale).astype(BF16)
                out_ref[dst, (SLOTS + h) * HD : (SLOTS + h + 1) * HD] = dk_s[h, pl.ds(place, run), :]
                out_ref[dst, (2 * SLOTS + h) * HD : (2 * SLOTS + h + 1) * HD] = dv_s[h, pl.ds(place, run), :]

    vmem = pl.BlockSpec(memory_space=pltpu.VMEM)
    return pl.pallas_call(
        kernel,
        out_shape=jax.ShapeDtypeStruct((seq, 3 * SLOTS * HD), BF16),
        in_specs=[pl.BlockSpec(memory_space=pltpu.SMEM), vmem, vmem, vmem, vmem],
        out_specs=vmem,
        scratch_shapes=[pltpu.VMEM((SLOTS, seq, HD), BF16)] * 4
        + [pltpu.VMEM((SLOTS, seq, HD), F32)]
        + [pltpu.VMEM((SLOTS, seq, HD), BF16)] * 2
        + [pltpu.VMEM((SLOTS, 1, seq), F32)],
        name="attend_back",
    )(meta, qkv, att, d_att, lse)


def on_device(groups):
    def run(tokens, doc_starts, pic_starts, ln1_gain, ln1_shift, w_qkv, bias_qv, w_attn, bias_attn,
            ln2_gain, ln2_shift, w_fc, bias_fc, w_proj, bias_proj, cotangent):
        y = lax.axis_index("y")
        x = lax.axis_index("x")
        z = lax.axis_index("z")
        c = lax.axis_index("c")
        chip = 2 * y + x
        rows, feat = tokens.shape
        docs, pics = doc_starts.shape[1], pic_starts.shape[1]
        ff = w_fc.shape[1]
        wrows = w_qkv.shape[0]
        hid = ff // 8
        sub = hid // 4
        width = SLOTS * HD
        last_start = feat - 2 * width
        chip_col = jnp.minimum(2 * width * chip, last_start)
        core_col = chip_col + width * c
        real = feat - 6 * width

        vec = jnp.concatenate([ln1_gain, ln1_shift, bias_qv, bias_attn, ln2_gain, ln2_shift, bias_fc, bias_proj])

        def head_columns(start):
            return jnp.concatenate(
                [lax.dynamic_slice_in_dim(w_qkv, k * feat + start, width, 1) for k in range(3)], axis=1
            )

        mine = head_columns(core_col)
        theirs = head_columns(chip_col + width * (1 - c))
        qkv_rows = jnp.concatenate(in_order2(mine, flip(theirs, "c"), c))
        vec = jnp.stack(in_order2(vec, flip(vec, "c"), c))
        vecs = jnp.stack(in_order([vec] + [z_flip(vec, m) for m in range(1, 4)], z)).reshape(8, -1)
        numbers = swap_planes(jnp.concatenate([doc_starts[0], pic_starts[0]]))
        step = feat // 4 // 128 * 128
        window = feat - 3 * step
        attn_cols = after(lax.dynamic_slice_in_dim(w_attn, step * chip, window, 1), vecs)
        attn_z = [attn_cols] + [z_flip(attn_cols, m) for m in range(1, 4)]
        attn_z = jnp.concatenate(in_order(attn_z, z))
        tok = swap_planes(after(tokens, vecs))
        mat_qkv = lax.all_gather(qkv_rows, "z", axis=0, tiled=True)

        def hidden_columns(core):
            return jnp.concatenate(
                [lax.dynamic_slice_in_dim(w_fc, hid * (2 * k + core) + sub * chip, sub, 1) for k in range(4)], axis=1
            )

        fc_rows = jnp.concatenate(in_order2(hidden_columns(c), flip(hidden_columns(1 - c), "c"), c))
        mat_fc = lax.all_gather(fc_rows, "z", axis=0, tiled=True)
        proj_rows = lax.dynamic_slice_in_dim(w_proj, sub * chip, sub, 0)
        mat_proj = lax.all_gather(proj_rows, "z", axis=0, tiled=True)

        def take(start, size):
            return vecs[:, start : start + size].astype(F32)

        gain_one = take(0, wrows).reshape(-1)
        shift_one = take(wrows, wrows).reshape(-1)
        bias_two = take(2 * wrows, 2 * wrows).reshape(2, feat)
        bias_out = take(4 * wrows, wrows).reshape(-1)
        gain_two = take(5 * wrows, wrows).reshape(-1)
        shift_two = take(6 * wrows, wrows).reshape(-1)
        bias_hidden = take(7 * wrows, hid).reshape(4, 2, 4, sub)
        bias_hidden = lax.dynamic_slice(bias_hidden, (0, c, chip, 0), (4, 1, 1, sub)).reshape(hid)
        bias_last = take(7 * wrows + hid, wrows).reshape(-1)
        bias_heads = lax.dynamic_slice(bias_two, (0, core_col), (2, width))
        bias_full = jnp.concatenate([bias_heads[0], jnp.zeros((width,), F32), bias_heads[1]])

        meta = jnp.concatenate([block_order(y, x, c), numbers])
        inputs = tok.astype(F32)
        normed_own = normalize(inputs, gain_one, shift_one).astype(BF16)
        n1_parts = gather_second(gather_first(normed_own))
        normed_one = join_rows(n1_parts)
        cot_own = swap_planes(after(cotangent, normed_own))
        attn_parts = chip_parts(after(attn_z, n1_parts[3], n1_parts[4]))
        qkv = (mul(normed_one, mat_qkv) + bias_full).astype(BF16)
        att, _, lse = attend(qkv, meta, docs, pics)
        cot_first = gather_first(after(cot_own, att))
        attn_mine = join_columns(attn_parts, after(chip, att), step)
        attn_theirs = flip(attn_mine, "c")
        att_rows = lax.all_to_all(att, ("y", "x", "c"), 0, 0, tiled=True).reshape(8, rows, width)
        att_own = jnp.concatenate(
            [att_rows[k] for k in range(6)] + [att_rows[7][:, width - real :]], axis=1
        )
        att_split = att_own.reshape(rows, 4, 2, wrows)
        att_even = att_split[:, :, 0].reshape(rows, feat // 2)
        att_odd = att_split[:, :, 1].reshape(rows, feat // 2)
        att_mine = jnp.where(c == 0, att_even, att_odd)
        att_theirs = jnp.where(c == 0, att_odd, att_even)
        middle = inputs + (mul(att_mine, attn_mine) + mul(att_theirs, attn_theirs)) + bias_out

        normed_two_own = normalize(middle, gain_two, shift_two).astype(BF16)
        cot_parts = gather_second(after(cot_first, att_own))
        n2_first = gather_first(normed_two_own)
        n2_parts = gather_second(n2_first)
        normed_two = join_rows(n2_parts)
        hidden = mul(normed_two, mat_fc) + bias_hidden
        activ = gelu_tanh(hidden).astype(BF16)
        cot = join_rows(after(cot_parts, activ))

        grad_in = cot_own.astype(F32)
        g_proj = cross(activ, cot).astype(BF16)
        d_activ = back_mul(after(cot, g_proj), mat_proj)
        _, gelu_pull = jax.vjp(gelu_tanh, hidden)
        d_hidden = gelu_pull(d_activ)[0].astype(BF16)
        g_fc = cross(normed_two, d_hidden).astype(BF16)
        g_proj = lax.psum_scatter(g_proj, "z", scatter_dimension=0, tiled=True)
        dn2_near, dn2_far = halves(after(d_hidden, g_fc), mat_fc, back_mul)
        g_fc = lax.psum_scatter(g_fc, "z", scatter_dimension=0, tiled=True)
        d_normed_two = scatter_sum(scatter_second(scatter_first(dn2_near, dn2_far, c), c))
        activ_late, d_hidden_late, _ = lax.optimization_barrier((activ, d_hidden, dn2_near))
        out_near, out_far = halves(activ_late, mat_proj, mul)
        g_bias_hidden = jnp.sum(d_hidden_late.astype(F32), axis=0)
        d_normed_two = after(d_normed_two, out_near)

        _, pull_two = jax.vjp(norm_plain, middle, gain_two)
        d_mid_norm, g_gain_two = pull_two(d_normed_two)
        g_shift_two = jnp.sum(d_normed_two, axis=0)
        d_middle = grad_in + d_mid_norm
        d_branch = d_middle.astype(BF16)
        g_bias_out = jnp.sum(d_branch.astype(F32), axis=0)

        d_mine = back_mul(d_branch, attn_mine).astype(BF16)
        d_theirs = back_mul(d_branch, attn_theirs).astype(BF16)
        d_even = jnp.where(c == 0, d_mine, d_theirs).reshape(rows, 4, 1, wrows)
        d_odd = jnp.where(c == 0, d_theirs, d_mine).reshape(rows, 4, 1, wrows)
        d_own = jnp.concatenate([d_even, d_odd], axis=2).reshape(rows, feat)
        d_rows = jnp.concatenate(
            [d_own[:, k * width : (k + 1) * width] for k in range(6)]
            + [jnp.zeros((rows, width), BF16)]
            + [jnp.concatenate([jnp.zeros((rows, width - real), BF16), d_own[:, 6 * width :]], axis=1)]
        )
        d_att = lax.all_to_all(d_rows, ("y", "x", "c"), 0, 0, tiled=True)
        out_first = scatter_first(out_near, after(out_far, d_rows), c)
        lse_rows = jnp.transpose(lse)[:, None, :]
        d_qkv = attend_back(qkv, att, d_att, lse_rows, after(meta, out_first[0]), docs, pics)
        branch_all = lax.all_gather(after(d_branch, d_qkv), ("y", "x", "c"), axis=0, tiled=True)
        dn1_near, dn1_far = halves(d_qkv, mat_qkv, back_mul)
        g_qkv = cross(normed_one, after(d_qkv, dn1_near)).astype(BF16)
        g_qkv_z = z_scatter_parts(g_qkv, z)
        dn1_second = scatter_second(scatter_first(dn1_near, dn1_far, c), c)
        d_normed_one = scatter_sum(after(dn1_second, g_qkv))

        _, pull_one = jax.vjp(norm_plain, inputs, gain_one)
        d_in_norm, g_gain_one = pull_one(d_normed_one)
        g_shift_one = jnp.sum(d_normed_one, axis=0)
        grad_own = (d_middle + d_in_norm).astype(BF16)
        tokens_grad = swap_planes(grad_own)

        out_second = scatter_second(out_first, after(c, dn1_second[1]))
        out_own = middle + scatter_sum(after(out_second, grad_own)) + bias_last
        output = swap_planes(out_own.astype(BF16))

        g_heads = cross(att, branch_all).astype(BF16)
        eighth = feat // 8
        g_heads = jnp.transpose(g_heads.reshape(width, 8, eighth), (1, 0, 2)).reshape(8 * width, eighth)
        g_heads = lax.all_to_all(g_heads, ("y", "x", "c"), 0, 0, tiled=True)
        g_attn = jnp.concatenate([g_heads[: 6 * width], g_heads[8 * width - real :]])
        g_attn_z = z_scatter_parts(g_attn, z)

        late_core = after(c, dn1_second[1], dn1_second[2])
        late_chip = after(chip, dn1_second[1], dn1_second[2])
        proj_parts = chip_parts(group_sum(g_proj, groups))
        fc_parts = chip_parts(core_rows([g_fc], late_core, groups))
        qkv_stack = core_rows(g_qkv_z, after(c, grad_own, g_attn), groups)
        qkv_parts = chip_parts(qkv_stack)
        attn_grads = chip_parts(core_rows(g_attn_z, after(c, qkv_stack), groups))

        w_proj_grad = assemble(
            proj_parts, late_chip, (ff // 8, feat), [(sub * at, 0, at, 0, sub, 0, feat) for at in range(4)]
        )
        w_fc_grad = assemble(
            fc_parts, late_chip, (wrows, ff),
            [
                (0, hid * (2 * k + core) + sub * at, at, core * wrows, wrows, k * sub, sub)
                for k in range(4) for core in range(2) for at in range(4)
            ],
        )
        w_attn_grad = assemble(
            attn_grads, late_chip, (wrows, feat),
            [(0, eighth * (2 * at + core), at, core * wrows, wrows, 0, eighth) for at in range(4) for core in range(2)],
        )
        places = []
        for k in range(3):
            for at in range(3):
                for core in range(2):
                    places.append((0, k * feat + width * (2 * at + core), at, core * wrows, wrows, k * width, width))
            places.append((0, (k + 1) * feat - real, 3, wrows, wrows, (k + 1) * width - real, real))
        w_qkv_grad = assemble(qkv_parts, chip, (wrows, 3 * feat), places)

        def by_row(*vectors):
            return [v.reshape(8, wrows) for v in vectors]

        hidden_slot = lax.dynamic_update_slice(
            jnp.zeros((4, 2, 4, sub), F32), g_bias_hidden.reshape(4, 1, 1, sub), (0, c, chip, 0)
        ).reshape(8, hid)
        g_bias_last = jnp.sum(grad_in, axis=0)
        d_qkv_sums = jnp.sum(d_qkv.astype(F32), axis=0)
        heads_slot = lax.dynamic_update_slice(
            jnp.zeros((2, feat), F32),
            jnp.stack([d_qkv_sums[:width], d_qkv_sums[2 * width :]]),
            (0, core_col),
        ).reshape(8, 2 * wrows)
        packed = jnp.concatenate(
            by_row(g_gain_one, g_shift_one, g_bias_out, g_gain_two, g_shift_two, g_bias_last) + [hidden_slot, heads_slot],
            axis=1,
        )
        sums = small_sum(after(packed, qkv_stack), z, c, chip, groups)
        e = [sums[k * wrows : (k + 1) * wrows] for k in range(6)]

        return (
            output, tokens_grad, e[0], e[1], w_qkv_grad, sums[6 * wrows + hid :], w_attn_grad,
            e[2], e[3], e[4], w_fc_grad, sums[6 * wrows : 6 * wrows + hid], w_proj_grad, e[5],
        )

    return run


def solution(mesh):
    reps = mesh.shape["rep"]
    line = mesh.shape["fsdp"]
    if reps % 4 or line != 8:
        raise ValueError("mesh")
    groups = reps // 4
    fine = Mesh(mesh.devices.reshape(groups, 2, 2, line // 2, 2), ("g", "y", "x", "z", "c"))
    every = ("g", "y", "x", "z", "c")
    rep = ("g", "y", "x")
    shard = ("z", "c")
    vec, mat, rowed = P(shard), P(shard, None), P(every, None)
    placed = (rowed, P(rep, None), P(rep, None), vec, vec, mat, vec, mat, vec, vec, vec, mat, vec, mat, vec, rowed)
    outs = (rowed, rowed, vec, vec, mat, vec, mat, vec, vec, vec, mat, vec, mat, vec)
    return jax.shard_map(on_device(groups), mesh=fine, in_specs=placed, out_specs=outs, check_vma=False)
```
